32 devices in a mesh: rows: 16 (over z, x, core), cols: 2 (over y).
Axes of the slice: x: 2, y: 2, z: 4, core: 2. Of those that a mesh axis runs over, the one named last changes fastest.
Arguments:
- kernel: float32 [16384, 1536], P('rows', 'cols'), may hold values from -0.15625 to 0.15625
- row_orbitals: float32 [16384, 512], P('rows', 'cols'), may hold values from -1.5 to 1.5
- col_orbitals: float32 [1536, 512], P('cols', 'rows'), may hold values from -1.5 to 1.5
- col_vectors: float32 [1536, 512], P('cols', 'rows'), may hold values from -6 to 6
Outputs:
- exchange: float32 [512, 16384], P('cols', 'rows')
The draws below stay inside these ranges and needn't reach their ends.
All inputs are finite; a program needn't handle non-finite values.
Results may differ from the reference program's by a relative error of at most 0.0003.
Values sent between devices are 32-bit elements; how exact they have to be, the bound alone decides.
A program may use at most 64 MiB of HBM per device.

```python
import jax
import jax.numpy as jnp
from jax import lax

NORB = 512
ROW_DEV = 1024
ROWS = 16384
COLS = 1536


def block_levels(rng, dims, cuts, low, largest):
    loudness = 1.0
    for axis_at, parts in cuts:
        steps = jax.random.uniform(jax.random.fold_in(jax.random.fold_in(rng, 6), axis_at), (parts,), jnp.float32, low / len(cuts), largest / len(cuts))
        loudness = loudness * jnp.repeat(jnp.exp(steps), dims[axis_at] // parts).reshape((-1,) + (1,) * (len(dims) - 1 - axis_at))
    return loudness


def centred(rng, extent, width, most, pieces=(), held_as=jnp.bfloat16):
    gain = block_levels(rng, extent, pieces, -0.22, 0.18) if pieces else 1.0
    entries = jax.random.normal(rng, extent, jnp.float32) * width * gain
    return jnp.minimum(jnp.maximum(entries, -most), most).astype(held_as)


def setup_inputs(seed: int = 0) -> dict:
    arg_keys = jax.random.split(jax.random.key(seed), 5)
    kernel = centred(arg_keys[0], (ROWS, COLS), COLS ** -0.5, 0.15625, ((0, 16), (1, 2)), jnp.float32)
    row_orbitals = centred(arg_keys[1], (ROWS, NORB), 0.21, 1.5, ((0, 16), (1, 2)), jnp.float32)
    col_orbitals = centred(arg_keys[2], (COLS, NORB), 0.21, 1.5, ((0, 2), (1, 16)), jnp.float32)
    col_vectors = centred(arg_keys[3], (COLS, NORB), 1.0, 6.0, ((0, 2), (1, 16)), jnp.float32)
    return {"kernel": kernel, "row_orbitals": row_orbitals, "col_orbitals": col_orbitals, "col_vectors": col_vectors}


def reference(kernel, row_orbitals, col_orbitals, col_vectors):
    block_rows = min(1024, ROW_DEV)
    count = ROWS // block_rows

    def one_block(index):
        start = (index * block_rows).astype(jnp.int32)
        kernel_rows = lax.dynamic_slice_in_dim(kernel, start, block_rows, 0)
        orbs = lax.dynamic_slice_in_dim(row_orbitals, start, block_rows, 0)
        gram = jnp.dot(orbs, col_orbitals.T, precision=lax.Precision.HIGHEST, preferred_element_type=jnp.float32)
        weighted = kernel_rows * gram
        return -jnp.dot(col_vectors.T, weighted.T, precision=lax.Precision.HIGHEST, preferred_element_type=jnp.float32)

    blocks = lax.map(one_block, jnp.arange(count, dtype=jnp.int32))
    return jnp.transpose(blocks, (1, 0, 2)).reshape(NORB, ROWS)
```

```python
import functools

import jax
import jax.numpy as jnp
from jax import lax
from jax.experimental import pallas as pl
from jax.experimental.pallas import tpu as pltpu
from jax.sharding import PartitionSpec as P

MESH = pl.DeviceIdType.MESH
LEFT, RIGHT, PAIR, CORE = range(4)


def split(x):
    hi = x.astype(jnp.bfloat16)
    return hi, (x - hi.astype(jnp.float32)).astype(jnp.bfloat16)


def dot3(a_hi, a_lo, b_hi, b_lo, dims):
    dot = functools.partial(lax.dot_general, dimension_numbers=(dims, ((), ())), preferred_element_type=jnp.float32)
    return dot(a_lo, b_hi) + dot(a_hi, b_lo) + dot(a_hi, b_hi)


def exchange_kernel(
    nr, nc, chunks,
    k_hbm, row_hbm, orb_hbm, vec_hbm, out_ref,
    k, rows, orb, vec, orb_hi, orb_lo, vec_hi, vec_lo, theirs, got, mine,
    local_sem, row_send, row_recv, col_send, col_recv, out_send, out_recv,
):
    r, c = lax.axis_index("rows"), lax.axis_index("cols")
    core, chip = lax.rem(r, 2), r // 2
    pair, line, lines = lax.rem(chip, 2), chip // 2, nr // 4
    per = orb_hbm.shape[0]
    chunk = row_hbm.shape[0] // chunks
    mb = row_hbm.shape[1]
    nb = theirs.shape[2]

    def at(l, p, q):
        return (l * 2 + p) * 2 + q

    goal = {
        LEFT: at(line - 1, pair, core),
        RIGHT: at(line + 1, pair, core),
        PAIR: at(line, 1 - pair, core),
        CORE: at(line, pair, 1 - core),
    }
    has_left, has_right = line > 0, line < lines - 1

    barrier = pltpu.get_barrier_semaphore()

    def greet(row, col):
        pl.semaphore_signal(barrier, inc=1, device_id=(row, col), device_id_type=MESH)

    for j in range(1, nc):
        greet(r, lax.rem(c + j, nc))
    greet(goal[PAIR], c)
    greet(goal[CORE], c)
    pl.when(has_left)(lambda: greet(goal[LEFT], c))
    pl.when(has_right)(lambda: greet(goal[RIGHT], c))

    k_copy = pltpu.make_async_copy(k_hbm, k, local_sem.at[0])
    row_copy = pltpu.make_async_copy(row_hbm, rows.at[0], local_sem.at[1])
    own = pl.ds(pl.multiple_of(r * per, per), per)
    orb_copy = pltpu.make_async_copy(orb_hbm, orb.at[own], local_sem.at[2])
    vec_copy = pltpu.make_async_copy(vec_hbm, vec.at[own], local_sem.at[3])
    for copy in (k_copy, row_copy, orb_copy, vec_copy):
        copy.start()

    pl.semaphore_wait(barrier, nc - 1 + 2 + has_left.astype(jnp.int32) + has_right.astype(jnp.int32))

    def row_chunk(j, i):
        at_rows = pl.ds(i * chunk, chunk) if isinstance(i, int) else pl.ds(pl.multiple_of(i * chunk, chunk), chunk)
        return pltpu.make_async_remote_copy(
            src_ref=row_hbm.at[at_rows],
            dst_ref=rows.at[j, at_rows],
            send_sem=row_send.at[j - 1, i],
            recv_sem=row_recv.at[j - 1, i],
            device_id=(r, lax.rem(c + j, nc)),
            device_id_type=MESH,
        )

    for i in range(chunks):
        for j in range(1, nc):
            row_chunk(j, i).start()

    def shard(t, s, way, first=False):
        full = (orb, vec)[t]
        there = full.at[pl.ds(pl.multiple_of(s * per, per), per)]
        return pltpu.make_async_remote_copy(
            src_ref=(orb_hbm, vec_hbm)[t] if first else there,
            dst_ref=there,
            send_sem=col_send.at[t, way, s],
            recv_sem=col_recv.at[t, s],
            device_id=(goal[way], c),
            device_id_type=MESH,
        )

    def line_sources(d):
        if d == 0:
            return [(line, None, ((LEFT, has_left), (RIGHT, has_right), (PAIR, None), (CORE, None)))]
        return [
            (line - d, line - d >= 0, ((RIGHT, has_right), (PAIR, None), (CORE, None))),
            (line + d, line + d < lines, ((LEFT, has_left), (PAIR, None), (CORE, None))),
        ]

    def when(cond, do):
        if cond is None:
            do()
        else:
            pl.when(cond)(do)

    def pass_on(op, t, d):
        for l, there, ways in line_sources(d):
            def go(l=l, ways=ways):
                s = at(l, pair, core)
                if op == "start" and d > 0:
                    shard(t, s, PAIR).wait_recv()
                for way, cond in ways:
                    copy = shard(t, s, way, d == 0)
                    when(cond, copy.start if op == "start" else copy.wait_send)
            when(there, go)

    def pass_over(op, t, d):
        for l, there, _ in line_sources(d):
            def go(l=l):
                s = at(l, 1 - pair, core)
                copy = shard(t, s, CORE)
                if op == "start":
                    copy.wait_recv()
                    copy.start()
                else:
                    copy.wait_send()
            when(there, go)

    for d in range(lines):
        for t in range(2):
            pass_on("start", t, d)
        if d > 0:
            for t in range(2):
                pass_over("start", t, d - 1)
    for t in range(2):
        pass_over("start", t, lines - 1)

    k_copy.wait()
    row_copy.wait()
    orb_copy.wait()
    vec_copy.wait()
    for t in range(2):
        for l in range(lines):
            for p in range(2):
                shard(t, at(l, p, 1 - core), CORE).wait_recv()

        @pl.loop(0, nr)
        def _(s, t=t):
            here = pl.ds(pl.multiple_of(s * per, per), per)
            if t == 0:
                orb_hi[here], orb_lo[here] = split(orb[here])
            else:
                vec_hi[here], vec_lo[here] = split(-vec[here])

    def out_chunk(j, i):
        return pltpu.make_async_remote_copy(
            src_ref=theirs.at[j - 1, i],
            dst_ref=got.at[j - 1, i],
            send_sem=out_send.at[j - 1, i],
            recv_sem=out_recv.at[j - 1, i],
            device_id=(r, lax.rem(c + j, nc)),
            device_id_type=MESH,
        )

    @pl.loop(0, chunks)
    def _(i):
        here = pl.ds(pl.multiple_of(i * chunk, chunk), chunk)
        gram = None
        for j in range(nc):
            if j > 0:
                row_chunk(j, i).wait_recv()
            block = pl.ds(pl.multiple_of(lax.rem(c - j + nc, nc) * mb, mb), mb)
            term = dot3(*split(rows[j, here, :]), orb_hi[block], orb_lo[block], ((1,), (0,)))
            gram = term if gram is None else gram + term
        w_hi, w_lo = split(k[here] * gram)
        for j in list(range(1, nc)) + [0]:
            block = pl.ds(pl.multiple_of(lax.rem(c + j, nc) * nb, nb), nb)
            part = dot3(vec_hi[block], vec_lo[block], w_hi, w_lo, ((1,), (1,)))
            if j == 0:
                mine[i] = part
            else:
                theirs[j - 1, i] = part
                out_chunk(j, i).start()

    for t in range(2):
        for d in range(lines):
            pass_on("wait", t, d)
            pass_over("wait", t, d)
    for i in range(chunks):
        for j in range(1, nc):
            row_chunk(j, i).wait_send()

    for i in range(chunks):
        total = mine[i]
        for j in range(1, nc):
            out_chunk(j, i).wait_recv()
            total = total + got[j - 1, i]
        out_ref[:, i * chunk:(i + 1) * chunk] = total
    for i in range(chunks):
        for j in range(1, nc):
            out_chunk(j, i).wait_send()


def solution(mesh):
    nr, nc = mesh.shape["rows"], mesh.shape["cols"]

    def body(kernel, row_orbitals, col_orbitals, col_vectors):
        n_rows, n_cols = kernel.shape
        mb, per = row_orbitals.shape[1], col_orbitals.shape[1]
        norb = mb * nc
        nb = norb // nc
        chunks = n_rows // 128
        chunk = n_rows // chunks
        f32, bf16, dma = jnp.float32, jnp.bfloat16, pltpu.SemaphoreType.DMA
        return pl.pallas_call(
            functools.partial(exchange_kernel, nr, nc, chunks),
            out_shape=jax.ShapeDtypeStruct((nb, n_rows), f32),
            in_specs=[pl.BlockSpec(memory_space=pl.ANY)] * 4,
            out_specs=pl.BlockSpec(memory_space=pltpu.VMEM),
            scratch_shapes=[
                pltpu.VMEM((n_rows, n_cols), f32),
                pltpu.VMEM((nc, n_rows, mb), f32),
                pltpu.VMEM((norb, n_cols), f32),
                pltpu.VMEM((norb, n_cols), f32),
                pltpu.VMEM((norb, n_cols), bf16),
                pltpu.VMEM((norb, n_cols), bf16),
                pltpu.VMEM((norb, n_cols), bf16),
                pltpu.VMEM((norb, n_cols), bf16),
                pltpu.VMEM((nc - 1, chunks, nb, chunk), f32),
                pltpu.VMEM((nc - 1, chunks, nb, chunk), f32),
                pltpu.VMEM((chunks, nb, chunk), f32),
                dma((4,)),
                dma((nc - 1, chunks)),
                dma((nc - 1, chunks)),
                dma((2, 4, nr)),
                dma((2, nr)),
                dma((nc - 1, chunks)),
                dma((nc - 1, chunks)),
            ],
            compiler_params=pltpu.CompilerParams(
                collective_id=0, has_side_effects=True, vmem_limit_bytes=60 * 1024 * 1024
            ),
        )(kernel, row_orbitals, col_orbitals.T, col_vectors.T)

    in_specs = (P("rows", "cols"), P("rows", "cols"), P("cols", "rows"), P("cols", "rows"))
    out_specs = P("cols", "rows")
    return jax.shard_map(body, mesh=mesh, in_specs=in_specs, out_specs=out_specs, check_vma=False)
```

```python
import functools

import jax
import jax.numpy as jnp
from jax import lax
from jax.experimental import pallas as pl
from jax.experimental.pallas import tpu as pltpu
from jax.sharding import PartitionSpec as P

MESH = pl.DeviceIdType.MESH
LEFT, RIGHT, PAIR, CORE = range(4)


def split(x):
    hi = x.astype(jnp.bfloat16)
    return hi, (x - hi.astype(jnp.float32)).astype(jnp.bfloat16)


def dot3(a_hi, a_lo, b_hi, b_lo, dims):
    dot = functools.partial(lax.dot_general, dimension_numbers=(dims, ((), ())), preferred_element_type=jnp.float32)
    return dot(a_lo, b_hi) + dot(a_hi, b_lo) + dot(a_hi, b_hi)


def exchange_kernel(
    nr, nc, chunks,
    k_hbm, row_hbm, orb_hbm, vec_hbm, out_ref,
    k, rows, orb, vec, orb_hi, orb_lo, vec_hi, vec_lo, theirs, got, mine,
    local_sem, row_send, row_recv, col_send, col_recv, out_send, out_recv,
):
    r, c = lax.axis_index("rows"), lax.axis_index("cols")
    core, chip = lax.rem(r, 2), r // 2
    pair, line, lines = lax.rem(chip, 2), chip // 2, nr // 4
    per = orb_hbm.shape[0]
    chunk = row_hbm.shape[0] // chunks
    mb = row_hbm.shape[1]
    nb = theirs.shape[2]

    def at(l, p, q):
        return (l * 2 + p) * 2 + q

    goal = {
        LEFT: at(line - 1, pair, core),
        RIGHT: at(line + 1, pair, core),
        PAIR: at(line, 1 - pair, core),
        CORE: at(line, pair, 1 - core),
    }
    has_left, has_right = line > 0, line < lines - 1

    barrier = pltpu.get_barrier_semaphore()

    def greet(row, col):
        pl.semaphore_signal(barrier, inc=1, device_id=(row, col), device_id_type=MESH)

    for j in range(1, nc):
        greet(r, lax.rem(c + j, nc))
    greet(goal[PAIR], c)
    greet(goal[CORE], c)
    pl.when(has_left)(lambda: greet(goal[LEFT], c))
    pl.when(has_right)(lambda: greet(goal[RIGHT], c))

    k_copy = pltpu.make_async_copy(k_hbm, k, local_sem.at[0])
    row_copy = pltpu.make_async_copy(row_hbm, rows.at[0], local_sem.at[1])
    own = pl.ds(pl.multiple_of(r * per, per), per)
    orb_copy = pltpu.make_async_copy(orb_hbm, orb.at[own], local_sem.at[2])
    vec_copy = pltpu.make_async_copy(vec_hbm, vec.at[own], local_sem.at[3])
    for copy in (k_copy, row_copy, orb_copy, vec_copy):
        copy.start()

    pl.semaphore_wait(barrier, nc - 1 + 2 + has_left.astype(jnp.int32) + has_right.astype(jnp.int32))

    def row_chunk(j, i):
        at_rows = pl.ds(i * chunk, chunk) if isinstance(i, int) else pl.ds(pl.multiple_of(i * chunk, chunk), chunk)
        return pltpu.make_async_remote_copy(
            src_ref=row_hbm.at[at_rows],
            dst_ref=rows.at[j, at_rows],
            send_sem=row_send.at[j - 1, i],
            recv_sem=row_recv.at[j - 1, i],
            device_id=(r, lax.rem(c + j, nc)),
            device_id_type=MESH,
        )

    for i in range(chunks):
        for j in range(1, nc):
            row_chunk(j, i).start()

    def shard(t, s, way, first=False):
        full = (orb, vec)[t]
        there = full.at[pl.ds(pl.multiple_of(s * per, per), per)]
        return pltpu.make_async_remote_copy(
            src_ref=(orb_hbm, vec_hbm)[t] if first else there,
            dst_ref=there,
            send_sem=col_send.at[t, way, s],
            recv_sem=col_recv.at[t, s],
            device_id=(goal[way], c),
            device_id_type=MESH,
        )

    def line_sources(d):
        if d == 0:
            return [(line, None, ((LEFT, has_left), (RIGHT, has_right), (PAIR, None), (CORE, None)))]
        return [
            (line - d, line - d >= 0, ((RIGHT, has_right), (PAIR, None), (CORE, None))),
            (line + d, line + d < lines, ((LEFT, has_left), (PAIR, None), (CORE, None))),
        ]

    def when(cond, do):
        if cond is None:
            do()
        else:
            pl.when(cond)(do)

    def pass_on(op, t, d):
        for l, there, ways in line_sources(d):
            def go(l=l, ways=ways):
                s = at(l, pair, core)
                if op == "start" and d > 0:
                    shard(t, s, PAIR).wait_recv()
                for way, cond in ways:
                    copy = shard(t, s, way, d == 0)
                    when(cond, copy.start if op == "start" else copy.wait_send)
            when(there, go)

    def pass_over(op, t, d):
        for l, there, _ in line_sources(d):
            def go(l=l):
                s = at(l, 1 - pair, core)
                copy = shard(t, s, CORE)
                if op == "start":
                    copy.wait_recv()
                    copy.start()
                else:
                    copy.wait_send()
            when(there, go)

    for d in range(lines):
        for t in range(2):
            pass_on("start", t, d)
        if d > 0:
            for t in range(2):
                pass_over("start", t, d - 1)
    for t in range(2):
        pass_over("start", t, lines - 1)

    k_copy.wait()
    row_copy.wait()
    orb_copy.wait()
    vec_copy.wait()
    for t in range(2):
        for l in range(lines):
            for p in range(2):
                shard(t, at(l, p, 1 - core), CORE).wait_recv()

        @pl.loop(0, nr)
        def _(s, t=t):
            here = pl.ds(pl.multiple_of(s * per, per), per)
            if t == 0:
                orb_hi[here], orb_lo[here] = split(orb[here])
            else:
                vec_hi[here], vec_lo[here] = split(-vec[here])

    def out_chunk(j, i):
        return pltpu.make_async_remote_copy(
            src_ref=theirs.at[j - 1, i],
            dst_ref=got.at[j - 1, i],
            send_sem=out_send.at[j - 1, i],
            recv_sem=out_recv.at[j - 1, i],
            device_id=(r, lax.rem(c + j, nc)),
            device_id_type=MESH,
        )

    @pl.loop(0, chunks)
    def _(i):
        here = pl.ds(pl.multiple_of(i * chunk, chunk), chunk)
        gram = None
        for j in range(nc):
            if j > 0:
                row_chunk(j, i).wait_recv()
            block = pl.ds(pl.multiple_of(lax.rem(c - j + nc, nc) * mb, mb), mb)
            term = dot3(*split(rows[j, here, :]), orb_hi[block], orb_lo[block], ((1,), (0,)))
            gram = term if gram is None else gram + term
        w_hi, w_lo = split(k[here] * gram)
        for j in list(range(1, nc)) + [0]:
            block = pl.ds(pl.multiple_of(lax.rem(c + j, nc) * nb, nb), nb)
            part = dot3(vec_hi[block], vec_lo[block], w_hi, w_lo, ((1,), (1,)))
            if j == 0:
                mine[i] = part
            else:
                theirs[j - 1, i] = part
                out_chunk(j, i).start()

    for t in range(2):
        for d in range(lines):
            pass_on("wait", t, d)
            pass_over("wait", t, d)
    for i in range(chunks):
        for j in range(1, nc):
            row_chunk(j, i).wait_send()

    for i in range(chunks):
        total = mine[i]
        for j in range(1, nc):
            out_chunk(j, i).wait_recv()
            total = total + got[j - 1, i]
        out_ref[:, i * chunk:(i + 1) * chunk] = total
    for i in range(chunks):
        for j in range(1, nc):
            out_chunk(j, i).wait_send()


def solution(mesh):
    nr, nc = mesh.shape["rows"], mesh.shape["cols"]

    def body(kernel, row_orbitals, col_orbitals, col_vectors):
        n_rows, n_cols = kernel.shape
        mb, per = row_orbitals.shape[1], col_orbitals.shape[1]
        norb = mb * nc
        nb = norb // nc
        chunks = n_rows // 128
        chunk = n_rows // chunks
        f32, bf16, dma = jnp.float32, jnp.bfloat16, pltpu.SemaphoreType.DMA
        return pl.pallas_call(
            functools.partial(exchange_kernel, nr, nc, chunks),
            out_shape=pltpu.VMEM((nb, n_rows), f32),
            in_specs=[pl.BlockSpec(memory_space=pl.ANY)] * 4,
            out_specs=pl.BlockSpec(memory_space=pltpu.VMEM),
            scratch_shapes=[
                pltpu.VMEM((n_rows, n_cols), f32),
                pltpu.VMEM((nc, n_rows, mb), f32),
                pltpu.VMEM((norb, n_cols), f32),
                pltpu.VMEM((norb, n_cols), f32),
                pltpu.VMEM((norb, n_cols), bf16),
                pltpu.VMEM((norb, n_cols), bf16),
                pltpu.VMEM((norb, n_cols), bf16),
                pltpu.VMEM((norb, n_cols), bf16),
                pltpu.VMEM((nc - 1, chunks, nb, chunk), f32),
                pltpu.VMEM((nc - 1, chunks, nb, chunk), f32),
                pltpu.VMEM((chunks, nb, chunk), f32),
                dma((4,)),
                dma((nc - 1, chunks)),
                dma((nc - 1, chunks)),
                dma((2, 4, nr)),
                dma((2, nr)),
                dma((nc - 1, chunks)),
                dma((nc - 1, chunks)),
            ],
            compiler_params=pltpu.CompilerParams(
                collective_id=0, has_side_effects=True, vmem_limit_bytes=60 * 1024 * 1024
            ),
        )(kernel, row_orbitals, col_orbitals.T, col_vectors.T)

    in_specs = (P("rows", "cols"), P("rows", "cols"), P("cols", "rows"), P("cols", "rows"))
    out_specs = P("cols", "rows")
    return jax.shard_map(body, mesh=mesh, in_specs=in_specs, out_specs=out_specs, check_vma=False)
```

```python
import functools

import jax
import jax.numpy as jnp
from jax import lax
from jax.experimental import pallas as pl
from jax.experimental.pallas import tpu as pltpu
from jax.sharding import PartitionSpec as P

MESH = pl.DeviceIdType.MESH
LEFT, RIGHT, PAIR, CORE = range(4)


def split(x):
    hi = x.astype(jnp.bfloat16)
    return hi, (x - hi.astype(jnp.float32)).astype(jnp.bfloat16)


def dot3(a_hi, a_lo, b_hi, b_lo, dims):
    dot = functools.partial(lax.dot_general, dimension_numbers=(dims, ((), ())), preferred_element_type=jnp.float32)
    return dot(a_lo, b_hi) + dot(a_hi, b_lo) + dot(a_hi, b_hi)


def exchange_kernel(
    nr, nc, chunks,
    k_hbm, row_hbm, orb_hbm, vec_hbm, out_ref,
    k, rows, orb, vec, orb_hi, orb_lo, vec_hi, vec_lo, theirs, got, mine,
    local_sem, row_send, row_recv, col_send, col_recv, core_recv, out_send, out_recv,
):
    r, c = lax.axis_index("rows"), lax.axis_index("cols")
    core, chip = lax.rem(r, 2), r // 2
    pair, line, lines = lax.rem(chip, 2), chip // 2, nr // 4
    per = orb_hbm.shape[0]
    chunk = row_hbm.shape[0] // chunks
    mb = row_hbm.shape[1]
    nb = theirs.shape[2]

    def at(l, p, q):
        return (l * 2 + p) * 2 + q

    goal = {
        LEFT: at(line - 1, pair, core),
        RIGHT: at(line + 1, pair, core),
        PAIR: at(line, 1 - pair, core),
        CORE: at(line, pair, 1 - core),
    }
    has_left, has_right = line > 0, line < lines - 1

    barrier = pltpu.get_barrier_semaphore()

    def greet(row, col):
        pl.semaphore_signal(barrier, inc=1, device_id=(row, col), device_id_type=MESH)

    for j in range(1, nc):
        greet(r, lax.rem(c + j, nc))
    greet(goal[PAIR], c)
    greet(goal[CORE], c)
    pl.when(has_left)(lambda: greet(goal[LEFT], c))
    pl.when(has_right)(lambda: greet(goal[RIGHT], c))

    k_copy = pltpu.make_async_copy(k_hbm, k, local_sem.at[0])
    row_copy = pltpu.make_async_copy(row_hbm, rows.at[0], local_sem.at[1])
    own = pl.ds(pl.multiple_of(r * per, per), per)
    orb_copy = pltpu.make_async_copy(orb_hbm, orb.at[own], local_sem.at[2])
    vec_copy = pltpu.make_async_copy(vec_hbm, vec.at[own], local_sem.at[3])
    for copy in (k_copy, row_copy, orb_copy, vec_copy):
        copy.start()

    pl.semaphore_wait(barrier, nc - 1 + 2 + has_left.astype(jnp.int32) + has_right.astype(jnp.int32))

    def row_chunk(j, i):
        at_rows = pl.ds(i * chunk, chunk) if isinstance(i, int) else pl.ds(pl.multiple_of(i * chunk, chunk), chunk)
        return pltpu.make_async_remote_copy(
            src_ref=row_hbm.at[at_rows],
            dst_ref=rows.at[j, at_rows],
            send_sem=row_send.at[j - 1],
            recv_sem=row_recv.at[j - 1, i],
            device_id=(r, lax.rem(c + j, nc)),
            device_id_type=MESH,
        )

    for i in range(chunks):
        for j in range(1, nc):
            row_chunk(j, i).start()

    def shard(t, l, p, way, first=False):
        there = (orb, vec)[t].at[pl.ds(pl.multiple_of(at(l, p, core) * per, per), per)]
        return pltpu.make_async_remote_copy(
            src_ref=(orb_hbm, vec_hbm)[t] if first else there,
            dst_ref=there,
            send_sem=col_send.at[way],
            recv_sem=core_recv.at[0] if way == CORE else col_recv.at[t, p, l],
            device_id=(goal[way], c),
            device_id_type=MESH,
        )

    def line_sources(d):
        if d == 0:
            return [(line, None, ((LEFT, has_left), (RIGHT, has_right), (PAIR, None), (CORE, None)))]
        return [
            (line - d, line - d >= 0, ((RIGHT, has_right), (PAIR, None), (CORE, None))),
            (line + d, line + d < lines, ((LEFT, has_left), (PAIR, None), (CORE, None))),
        ]

    def when(cond, do):
        if cond is None:
            do()
        else:
            pl.when(cond)(do)

    def pass_on(t, d):
        for l, there, ways in line_sources(d):
            def go(l=l, ways=ways):
                if d > 0:
                    shard(t, l, pair, PAIR).wait_recv()
                for way, cond in ways:
                    when(cond, shard(t, l, pair, way, d == 0).start)
            when(there, go)

    def pass_over(t, d):
        for l, there, _ in line_sources(d):
            def go(l=l):
                shard(t, l, 1 - pair, PAIR).wait_recv()
                shard(t, l, 1 - pair, CORE).start()
            when(there, go)

    for d in range(lines):
        for t in range(2):
            pass_on(t, d)
        if d > 0:
            for t in range(2):
                pass_over(t, d - 1)
    for t in range(2):
        pass_over(t, lines - 1)

    def bulk(way, count):
        part = orb.at[pl.ds(0, count * per)]
        return pltpu.make_async_remote_copy(
            src_ref=part,
            dst_ref=part,
            send_sem=col_send.at[way],
            recv_sem=core_recv.at[0],
            device_id=(goal[CORE], c),
            device_id_type=MESH,
        )

    k_copy.wait()
    row_copy.wait()
    orb_copy.wait()
    vec_copy.wait()
    bulk(CORE, nr).wait_recv()
    for t in range(2):

        @pl.loop(0, nr)
        def _(s, t=t):
            here = pl.ds(pl.multiple_of(s * per, per), per)
            if t == 0:
                orb_hi[here], orb_lo[here] = split(orb[here])
            else:
                vec_hi[here], vec_lo[here] = split(-vec[here])

    def out_chunk(j, i):
        return pltpu.make_async_remote_copy(
            src_ref=theirs.at[j - 1, i],
            dst_ref=got.at[j - 1, i],
            send_sem=out_send.at[j - 1],
            recv_sem=out_recv.at[j - 1, i],
            device_id=(r, lax.rem(c + j, nc)),
            device_id_type=MESH,
        )

    @pl.loop(0, chunks)
    def _(i):
        here = pl.ds(pl.multiple_of(i * chunk, chunk), chunk)
        gram = None
        for j in range(nc):
            if j > 0:
                row_chunk(j, i).wait_recv()
            block = pl.ds(pl.multiple_of(lax.rem(c - j + nc, nc) * mb, mb), mb)
            term = dot3(*split(rows[j, here, :]), orb_hi[block], orb_lo[block], ((1,), (0,)))
            gram = term if gram is None else gram + term
        w_hi, w_lo = split(k[here] * gram)
        for j in list(range(1, nc)) + [0]:
            block = pl.ds(pl.multiple_of(lax.rem(c + j, nc) * nb, nb), nb)
            part = dot3(vec_hi[block], vec_lo[block], w_hi, w_lo, ((1,), (1,)))
            if j == 0:
                mine[i] = part
            else:
                theirs[j - 1, i] = part
                out_chunk(j, i).start()

    bulk(PAIR, 2 * lines).wait_send()
    bulk(CORE, nr).wait_send()
    for l in range(lines):
        if l > 0:
            pl.when(line == l)(bulk(LEFT, 2 * (lines - l)).wait_send)
        if l < lines - 1:
            pl.when(line == l)(bulk(RIGHT, 2 * (l + 1)).wait_send)

    for i in range(chunks):
        total = mine[i]
        for j in range(1, nc):
            out_chunk(j, i).wait_recv()
            total = total + got[j - 1, i]
        out_ref[:, i * chunk:(i + 1) * chunk] = total
    for j in range(1, nc):
        peer = {"device_id": (r, lax.rem(c + j, nc)), "device_id_type": MESH}
        pltpu.make_async_remote_copy(
            row_hbm, rows.at[j], row_send.at[j - 1], row_recv.at[j - 1, 0], **peer
        ).wait_send()
        pltpu.make_async_remote_copy(
            theirs.at[j - 1], got.at[j - 1], out_send.at[j - 1], out_recv.at[j - 1, 0], **peer
        ).wait_send()


def solution(mesh):
    nr, nc = mesh.shape["rows"], mesh.shape["cols"]

    def body(kernel, row_orbitals, col_orbitals, col_vectors):
        n_rows, n_cols = kernel.shape
        mb, per = row_orbitals.shape[1], col_orbitals.shape[1]
        norb = mb * nc
        nb = norb // nc
        chunks = n_rows // 128
        chunk = n_rows // chunks
        f32, bf16, dma = jnp.float32, jnp.bfloat16, pltpu.SemaphoreType.DMA
        return pl.pallas_call(
            functools.partial(exchange_kernel, nr, nc, chunks),
            out_shape=pltpu.VMEM((nb, n_rows), f32),
            in_specs=[pl.BlockSpec(memory_space=pl.ANY)] * 4,
            out_specs=pl.BlockSpec(memory_space=pltpu.VMEM),
            scratch_shapes=[
                pltpu.VMEM((n_rows, n_cols), f32),
                pltpu.VMEM((nc, n_rows, mb), f32),
                pltpu.VMEM((norb, n_cols), f32),
                pltpu.VMEM((norb, n_cols), f32),
                pltpu.VMEM((norb, n_cols), bf16),
                pltpu.VMEM((norb, n_cols), bf16),
                pltpu.VMEM((norb, n_cols), bf16),
                pltpu.VMEM((norb, n_cols), bf16),
                pltpu.VMEM((nc - 1, chunks, nb, chunk), f32),
                pltpu.VMEM((nc - 1, chunks, nb, chunk), f32),
                pltpu.VMEM((chunks, nb, chunk), f32),
                dma((4,)),
                dma((nc - 1,)),
                dma((nc - 1, chunks)),
                dma((4,)),
                dma((2, 2, nr // 4)),
                dma((1,)),
                dma((nc - 1,)),
                dma((nc - 1, chunks)),
            ],
            compiler_params=pltpu.CompilerParams(
                collective_id=0, has_side_effects=True, vmem_limit_bytes=60 * 1024 * 1024
            ),
        )(kernel, row_orbitals, col_orbitals.T, col_vectors.T)

    in_specs = (P("rows", "cols"), P("rows", "cols"), P("cols", "rows"), P("cols", "rows"))
    out_specs = P("cols", "rows")
    return jax.shard_map(body, mesh=mesh, in_specs=in_specs, out_specs=out_specs, check_vma=False)
```

```python
import functools

import jax
import jax.numpy as jnp
from jax import lax
from jax.experimental import pallas as pl
from jax.experimental.pallas import tpu as pltpu
from jax.sharding import PartitionSpec as P

MESH = pl.DeviceIdType.MESH
LEFT, RIGHT, PAIR, CORE = range(4)


def split(x):
    hi = x.astype(jnp.bfloat16)
    return hi, (x - hi.astype(jnp.float32)).astype(jnp.bfloat16)


def dot3(a_hi, a_lo, b_hi, b_lo, dims):
    dot = functools.partial(lax.dot_general, dimension_numbers=(dims, ((), ())), preferred_element_type=jnp.float32)
    return dot(a_lo, b_hi) + dot(a_hi, b_lo) + dot(a_hi, b_hi)


def exchange_kernel(
    nr, nc, chunks,
    k_hbm, row_hbm, orb_hbm, vec_hbm, out_ref,
    k, rows, orb, vec, orb_hi, orb_lo, vec_hi, vec_lo, theirs, got, mine,
    local_sem, row_send, row_recv, col_send, col_recv, core_recv, out_send, out_recv,
):
    r, c = lax.axis_index("rows"), lax.axis_index("cols")
    core, chip = lax.rem(r, 2), r // 2
    pair, line, lines = lax.rem(chip, 2), chip // 2, nr // 4
    per = orb_hbm.shape[0]
    chunk = row_hbm.shape[0] // chunks
    mb = row_hbm.shape[1]
    nb = theirs.shape[2]

    def at(l, p, q):
        return (l * 2 + p) * 2 + q

    goal = {
        LEFT: at(line - 1, pair, core),
        RIGHT: at(line + 1, pair, core),
        PAIR: at(line, 1 - pair, core),
        CORE: at(line, pair, 1 - core),
    }
    has_left, has_right = line > 0, line < lines - 1

    barrier = pltpu.get_barrier_semaphore()

    def greet(row, col):
        pl.semaphore_signal(barrier, inc=1, device_id=(row, col), device_id_type=MESH)

    for j in range(1, nc):
        greet(r, lax.rem(c + j, nc))
    greet(goal[PAIR], c)
    greet(goal[CORE], c)
    pl.when(has_left)(lambda: greet(goal[LEFT], c))
    pl.when(has_right)(lambda: greet(goal[RIGHT], c))

    k_copy = pltpu.make_async_copy(k_hbm, k, local_sem.at[0])
    row_copy = pltpu.make_async_copy(row_hbm, rows.at[0], local_sem.at[1])
    own = pl.ds(pl.multiple_of(r * per, per), per)
    orb_copy = pltpu.make_async_copy(orb_hbm, orb.at[own], local_sem.at[2])
    vec_copy = pltpu.make_async_copy(vec_hbm, vec.at[own], local_sem.at[3])
    for copy in (k_copy, row_copy, orb_copy, vec_copy):
        copy.start()

    pl.semaphore_wait(barrier, nc - 1 + 2 + has_left.astype(jnp.int32) + has_right.astype(jnp.int32))

    def row_chunk(j, i):
        at_rows = pl.ds(i * chunk, chunk) if isinstance(i, int) else pl.ds(pl.multiple_of(i * chunk, chunk), chunk)
        return pltpu.make_async_remote_copy(
            src_ref=row_hbm.at[at_rows],
            dst_ref=rows.at[j, at_rows],
            send_sem=row_send.at[j - 1],
            recv_sem=row_recv.at[j - 1, i],
            device_id=(r, lax.rem(c + j, nc)),
            device_id_type=MESH,
        )

    for i in range(chunks):
        for j in range(1, nc):
            row_chunk(j, i).start()

    def shard(t, l, p, way, first=False):
        there = (orb, vec)[t].at[pl.ds(pl.multiple_of(at(l, p, core) * per, per), per)]
        return pltpu.make_async_remote_copy(
            src_ref=(orb_hbm, vec_hbm)[t] if first else there,
            dst_ref=there,
            send_sem=col_send.at[way],
            recv_sem=core_recv.at[0] if way == CORE else col_recv.at[t, p, l],
            device_id=(goal[way], c),
            device_id_type=MESH,
        )

    def line_sources(d):
        if d == 0:
            return [(line, None, ((LEFT, has_left), (RIGHT, has_right), (PAIR, None), (CORE, None)))]
        return [
            (line - d, line - d >= 0, ((RIGHT, has_right), (PAIR, None), (CORE, None))),
            (line + d, line + d < lines, ((LEFT, has_left), (PAIR, None), (CORE, None))),
        ]

    def when(cond, do):
        if cond is None:
            do()
        else:
            pl.when(cond)(do)

    def keep(t, s):
        here = pl.ds(pl.multiple_of(s * per, per), per)
        if t == 0:
            orb_hi[here], orb_lo[here] = split(orb[here])
        else:
            vec_hi[here], vec_lo[here] = split(-vec[here])

    def pass_on(t, d):
        for l, there, ways in line_sources(d):
            def go(l=l, ways=ways):
                if d > 0:
                    shard(t, l, pair, PAIR).wait_recv()
                for way, cond in ways:
                    when(cond, shard(t, l, pair, way, d == 0).start)
                if d > 0:
                    keep(t, at(l, pair, core))
            when(there, go)

    def pass_over(t, d):
        for l, there, _ in line_sources(d):
            def go(l=l):
                shard(t, l, 1 - pair, PAIR).wait_recv()
                shard(t, l, 1 - pair, CORE).start()
                keep(t, at(l, 1 - pair, core))
            when(there, go)

    for d in range(lines):
        for t in range(2):
            pass_on(t, d)
        if d > 0:
            for t in range(2):
                pass_over(t, d - 1)
    for t in range(2):
        pass_over(t, lines - 1)

    def bulk(way, count):
        part = orb.at[pl.ds(0, count * per)]
        return pltpu.make_async_remote_copy(
            src_ref=part,
            dst_ref=part,
            send_sem=col_send.at[way],
            recv_sem=core_recv.at[0],
            device_id=(goal[CORE], c),
            device_id_type=MESH,
        )

    for copy in (orb_copy, vec_copy, k_copy, row_copy):
        copy.wait()
    for t in range(2):
        keep(t, r)
    bulk(CORE, nr).wait_recv()
    for t in range(2):

        @pl.loop(0, nr // 2)
        def _(m, t=t):
            keep(t, m * 2 + 1 - core)

    def out_chunk(j, i):
        return pltpu.make_async_remote_copy(
            src_ref=theirs.at[j - 1, i],
            dst_ref=got.at[j - 1, i],
            send_sem=out_send.at[j - 1],
            recv_sem=out_recv.at[j - 1, i],
            device_id=(r, lax.rem(c + j, nc)),
            device_id_type=MESH,
        )

    @pl.loop(0, chunks)
    def _(i):
        here = pl.ds(pl.multiple_of(i * chunk, chunk), chunk)
        gram = None
        for j in range(nc):
            if j > 0:
                row_chunk(j, i).wait_recv()
            block = pl.ds(pl.multiple_of(lax.rem(c - j + nc, nc) * mb, mb), mb)
            term = dot3(*split(rows[j, here, :]), orb_hi[block], orb_lo[block], ((1,), (0,)))
            gram = term if gram is None else gram + term
        w_hi, w_lo = split(k[here] * gram)
        for j in list(range(1, nc)) + [0]:
            block = pl.ds(pl.multiple_of(lax.rem(c + j, nc) * nb, nb), nb)
            part = dot3(vec_hi[block], vec_lo[block], w_hi, w_lo, ((1,), (1,)))
            if j == 0:
                mine[i] = part
            else:
                theirs[j - 1, i] = part
                out_chunk(j, i).start()

    bulk(PAIR, 2 * lines).wait_send()
    bulk(CORE, nr).wait_send()
    for l in range(lines):
        if l > 0:
            pl.when(line == l)(bulk(LEFT, 2 * (lines - l)).wait_send)
        if l < lines - 1:
            pl.when(line == l)(bulk(RIGHT, 2 * (l + 1)).wait_send)

    for i in range(chunks):
        total = mine[i]
        for j in range(1, nc):
            out_chunk(j, i).wait_recv()
            total = total + got[j - 1, i]
        out_ref[:, i * chunk:(i + 1) * chunk] = total
    for j in range(1, nc):
        peer = {"device_id": (r, lax.rem(c + j, nc)), "device_id_type": MESH}
        pltpu.make_async_remote_copy(
            row_hbm, rows.at[j], row_send.at[j - 1], row_recv.at[j - 1, 0], **peer
        ).wait_send()
        pltpu.make_async_remote_copy(
            theirs.at[j - 1], got.at[j - 1], out_send.at[j - 1], out_recv.at[j - 1, 0], **peer
        ).wait_send()


def solution(mesh):
    nr, nc = mesh.shape["rows"], mesh.shape["cols"]

    def body(kernel, row_orbitals, col_orbitals, col_vectors):
        n_rows, n_cols = kernel.shape
        mb, per = row_orbitals.shape[1], col_orbitals.shape[1]
        norb = mb * nc
        nb = norb // nc
        chunks = n_rows // 256
        chunk = n_rows // chunks
        f32, bf16, dma = jnp.float32, jnp.bfloat16, pltpu.SemaphoreType.DMA
        return pl.pallas_call(
            functools.partial(exchange_kernel, nr, nc, chunks),
            out_shape=pltpu.VMEM((nb, n_rows), f32),
            in_specs=[pl.BlockSpec(memory_space=pl.ANY)] * 4,
            out_specs=pl.BlockSpec(memory_space=pltpu.VMEM),
            scratch_shapes=[
                pltpu.VMEM((n_rows, n_cols), f32),
                pltpu.VMEM((nc, n_rows, mb), f32),
                pltpu.VMEM((norb, n_cols), f32),
                pltpu.VMEM((norb, n_cols), f32),
                pltpu.VMEM((norb, n_cols), bf16),
                pltpu.VMEM((norb, n_cols), bf16),
                pltpu.VMEM((norb, n_cols), bf16),
                pltpu.VMEM((norb, n_cols), bf16),
                pltpu.VMEM((nc - 1, chunks, nb, chunk), f32),
                pltpu.VMEM((nc - 1, chunks, nb, chunk), f32),
                pltpu.VMEM((chunks, nb, chunk), f32),
                dma((4,)),
                dma((nc - 1,)),
                dma((nc - 1, chunks)),
                dma((4,)),
                dma((2, 2, nr // 4)),
                dma((1,)),
                dma((nc - 1,)),
                dma((nc - 1, chunks)),
            ],
            compiler_params=pltpu.CompilerParams(
                collective_id=0, has_side_effects=True, vmem_limit_bytes=60 * 1024 * 1024
            ),
        )(kernel, row_orbitals, col_orbitals.T, col_vectors.T)

    in_specs = (P("rows", "cols"), P("rows", "cols"), P("cols", "rows"), P("cols", "rows"))
    out_specs = P("cols", "rows")
    return jax.shard_map(body, mesh=mesh, in_specs=in_specs, out_specs=out_specs, check_vma=False)
```
